256 devices in a mesh: batch: 32 (over y, x, core), seq: 8 (over z).
Axes of the slice: x: 4, y: 4, z: 8, core: 2. Of those that a mesh axis runs over, the one named last changes fastest.
Arguments:
- query_rows: bfloat16 [32, 2560, 3072], P('batch', 'seq'), may hold values from -16 to 16
- key_rows: bfloat16 [32, 2560, 3072], P('batch', 'seq'), may hold values from -16 to 16
- value_rows: bfloat16 [32, 2560, 3072], P('batch', 'seq'), may hold values from -10 to 10
- cached_rows: bfloat16 [32, 2560, 3072], P('batch', 'seq'), may hold values from -4 to 4
- plan: int32 [32, 28], replicated, may hold values from 0 to 1, as said below
- timestep: int32 [32], replicated, may hold values from 0 to 27
- assignment: int32 [32], replicated, may hold values from 0 to 31, as said below
Outputs:
- refreshed: bfloat16 [32, 2560, 3072], P('batch', 'seq')
The draws below stay inside these ranges and needn't reach their ends.
Inputs may be any that keep to these rules, and one draw needn't show every extreme that they name: plan[r, t] is 1 for t = 0 and for the timesteps at which request r refreshes, every 3 timesteps from its own offset, else 0. `assignment`: a permutation of the requests; of the two slots g and g + 16, exactly one holds a request with active = 1.
All inputs are finite; a program needn't handle non-finite values.
Results may differ from the reference program's by a relative error of at most 0.0025.
Values may be sent and summed in bfloat16 or wider, within the bound.
No kernel may reach another device: no remote copies, remote signals or barrier semaphores. Data moves between devices by JAX's collectives and lax.ppermute only.
A program may use at most 128 MiB of HBM per device.

```python
import math
import jax
import jax.numpy as jnp
from jax import lax

HEADS = 24
HEAD_DIM = 128
D = 3072
SEQ_LEN = 2560
STEPS = 28
CACHE_EVERY = 3
REQUESTS = 32


def fora_tables(key):
    halfway = REQUESTS // 2
    base_key = jax.random.fold_in(key, 4242)
    order_seed, coin_seed, phase_seed, pick_seed = jax.random.split(base_key, 4)
    slot_order = jax.random.permutation(order_seed, REQUESTS).astype(jnp.int32)
    coin_flips = jax.random.randint(coin_seed, (halfway,), 0, 2).astype(jnp.int32)
    slot_full = jnp.concatenate([coin_flips, 1 - coin_flips])
    request_full = jnp.zeros((REQUESTS,), jnp.int32).at[slot_order].set(slot_full)
    phases = jax.random.randint(phase_seed, (REQUESTS,), 0, CACHE_EVERY).astype(jnp.int32)
    first_slot = jnp.where(coin_flips[0] == 1, 0, halfway)
    second_slot = jnp.where(coin_flips[1] == 1, 1, 1 + halfway)
    first_request = slot_order[first_slot]
    second_request = slot_order[second_slot]
    phases = phases.at[second_request].set(0)
    pick_values = jax.random.randint(pick_seed, (REQUESTS,), 0, 1 << 20).astype(jnp.int32)
    full_room = (STEPS - 1 + phases) // CACHE_EVERY
    reuse_room = (STEPS - 2 + phases) // CACHE_EVERY
    full_time = CACHE_EVERY * (1 + pick_values % full_room) - phases
    reuse_time = CACHE_EVERY * (1 + pick_values % reuse_room) - phases + 1
    step_times = jnp.where(request_full == 1, full_time, reuse_time).astype(jnp.int32)
    step_times = step_times.at[first_request].set(0).at[second_request].set(STEPS - 1)
    step_grid = jnp.arange(STEPS, dtype=jnp.int32)[None, :]
    refresh = (step_grid == 0) | ((step_grid + phases[:, None]) % CACHE_EVERY == 0)
    return (refresh.astype(jnp.int32), step_times, slot_order)


def draw_plan(key, part):
    return fora_tables(key)[0]


def draw_timestep(key, part):
    return fora_tables(key)[1]


def draw_assignment(key, part):
    return fora_tables(key)[2]


def query_key_pair(key):
    base_key = jax.random.fold_in(key, 777)
    query_seed, key_seed = jax.random.split(base_key, 2)
    queries = jnp.clip(1.41 * jax.random.normal(query_seed, (REQUESTS, SEQ_LEN, D), jnp.float32), -16.0, 16.0)
    keyrows = jnp.clip(1.41 * jax.random.normal(key_seed, (REQUESTS, SEQ_LEN, D), jnp.float32), -16.0, 16.0)
    return (queries, keyrows)


def draw_query_rows(key, part):
    return query_key_pair(key)[0].astype(jnp.bfloat16)


def draw_key_rows(key, part):
    return query_key_pair(key)[1].astype(jnp.bfloat16)


def levels(key, shape, cuts, smallest, top_value):
    factor_of = 1.0
    for dim, shards_of in cuts:
        heights = jax.random.uniform(jax.random.fold_in(jax.random.fold_in(key, 6), dim), (shards_of,), jnp.float32, smallest / len(cuts), top_value / len(cuts))
        factor_of = factor_of * jnp.repeat(jnp.exp(heights), shape[dim] // shards_of).reshape((-1,) + (1,) * (len(shape) - 1 - dim))
    return factor_of


def gaussian(stream_key, dims, scale, bound, pieces=(), kind=jnp.bfloat16):
    drawn = scale * jax.random.normal(stream_key, dims, jnp.float32)
    if pieces:
        drawn = drawn * levels(stream_key, dims, pieces, -0.22, 0.18)
    return jnp.clip(drawn, -bound, bound).astype(kind)


def setup_inputs(seed: int = 0) -> dict:
    splits = jax.random.split(jax.random.key(seed), 8)
    query_rows = draw_query_rows(jax.random.fold_in(splits[7], 71), 0)
    key_rows = draw_key_rows(jax.random.fold_in(splits[7], 71), 0)
    value_rows = gaussian(splits[2], (REQUESTS, SEQ_LEN, D), 2.0, 10.0, ((0, 32), (1, 8)))
    cached_rows = gaussian(splits[3], (REQUESTS, SEQ_LEN, D), 0.5, 4.0, ((0, 32), (1, 8)))
    plan = draw_plan(jax.random.fold_in(splits[7], 71), 0)
    timestep = draw_timestep(jax.random.fold_in(splits[7], 71), 0)
    assignment = draw_assignment(jax.random.fold_in(splits[7], 71), 0)
    return dict(query_rows=query_rows, key_rows=key_rows, value_rows=value_rows, cached_rows=cached_rows, plan=plan, timestep=timestep, assignment=assignment)


def attend_head(inputs):
    head_queries, head_keys, head_values = inputs
    factor = 1.0 / math.sqrt(head_queries.shape[-1])
    scores = jnp.dot(head_queries, head_keys.T, preferred_element_type=jnp.float32) * factor
    peak = lax.optimization_barrier(jnp.max(scores, axis=1, keepdims=True))
    shifted = jnp.exp(scores - peak)
    total = lax.optimization_barrier(jnp.sum(shifted, axis=1, keepdims=True))
    weights = shifted.astype(jnp.bfloat16)
    mixed = jnp.dot(weights, head_values, preferred_element_type=jnp.float32)
    return (mixed / total).astype(jnp.bfloat16)

def attend_request(query_rows, key_rows, value_rows):

    def split_heads(rows):
        return jnp.transpose(rows.reshape(SEQ_LEN, HEADS, HEAD_DIM), (1, 0, 2))
    heads_out = lax.map(attend_head, (split_heads(query_rows), split_heads(key_rows), split_heads(value_rows)))
    return jnp.transpose(heads_out, (1, 0, 2)).reshape(SEQ_LEN, HEADS * HEAD_DIM)

def reference(query_rows, key_rows, value_rows, cached_rows, plan, timestep, assignment):
    active = plan[assignment, timestep[assignment]] > 0

    def per_slot(inputs):
        slot_queries, slot_keys, slot_values, slot_cache, slot_flag = inputs

        def fresh(unused):
            return attend_request(slot_queries, slot_keys, slot_values)

        def reuse(unused):
            return slot_cache
        return lax.cond(slot_flag, fresh, reuse, 0)
    return lax.map(per_slot, (query_rows, key_rows, value_rows, cached_rows, active))
```

```python
import functools
import math

import jax
import jax.numpy as jnp
from jax import lax
from jax.experimental import pallas as pl
from jax.experimental.pallas import tpu as pltpu
from jax.sharding import PartitionSpec as P

HEAD_DIM = 128
GROUPS = 3
VMEM_LIMIT = 48 << 20

ANY = pl.BlockSpec(memory_space=pl.ANY)
SMEM = pl.BlockSpec(memory_space=pltpu.SMEM)


def params():
    return pltpu.CompilerParams(vmem_limit_bytes=VMEM_LIMIT)


def ring(pieces):
    order = [0]
    for step in range(1, pieces // 2):
        order += [step, pieces - step]
    if pieces > 1:
        order.append(pieces // 2)
    return order


def head_columns(me, offset, group, pieces):
    head = group * pieces + lax.rem(me + offset, pieces)
    return pl.ds(pl.multiple_of(head * HEAD_DIM, HEAD_DIM), HEAD_DIM)


def run_copies(copies):
    for copy in copies:
        copy.start()
    for copy in copies:
        copy.wait()


def pack_kernel(pieces, group, *refs):
    sources, outs, sems = refs[:3], refs[3 : 3 + pieces], refs[3 + pieces]
    me = lax.axis_index("seq")
    run_copies(
        [
            pltpu.make_async_copy(
                sources[part].at[0, :, head_columns(me, offset, group, pieces)],
                outs[offset].at[part],
                sems.at[offset, part],
            )
            for offset in range(pieces)
            for part in range(3)
        ]
    )


def pack_far_kernel(pieces, group, assignment, timestep, plan, *refs):
    sources, out, flag, sems = refs[:3], refs[3], refs[4], refs[5]
    me = lax.axis_index("seq")
    slot = lax.axis_index("batch")
    request = assignment[slot]
    flag[0] = plan[request, timestep[request]]
    run_copies(
        [
            pltpu.make_async_copy(
                sources[part].at[0, :, head_columns(me, offset, group, pieces)],
                out.at[offset, part],
                sems.at[offset, part],
            )
            for offset in range(pieces)
            for part in range(3)
        ]
    )


def pack_second_kernel(pieces, group, flag, *refs):
    sources, far = refs[:3], refs[3]
    pairs, queries = refs[4 : 4 + pieces], refs[4 + pieces : 4 + 2 * pieces]
    sems = refs[4 + 2 * pieces]
    me = lax.axis_index("seq")

    def target(offset, part):
        return queries[offset] if part == 0 else pairs[offset].at[part - 1]

    @pl.when(flag[0] > 0)
    def _():
        run_copies(
            [
                pltpu.make_async_copy(
                    sources[part].at[0, :, head_columns(me, offset, group, pieces)],
                    target(offset, part),
                    sems.at[offset, part],
                )
                for offset in range(pieces)
                for part in range(3)
            ]
        )

    @pl.when(flag[0] <= 0)
    def _():
        run_copies(
            [
                pltpu.make_async_copy(far.at[offset, part], target(offset, part), sems.at[offset, part])
                for offset in range(pieces)
                for part in range(3)
            ]
        )


def attend_block(query, keys, values):
    factor = math.log2(math.e) / math.sqrt(HEAD_DIM)
    scores = lax.dot_general(
        query, keys[...], (((1,), (1,)), ((), ())), preferred_element_type=jnp.float32
    )
    peak = jnp.max(scores, axis=1, keepdims=True)
    shifted = jnp.exp2((scores - peak) * factor)
    total = jnp.sum(shifted, axis=1, keepdims=True)
    mixed = jnp.dot(
        shifted.astype(jnp.bfloat16), values[...], preferred_element_type=jnp.float32
    )
    return (mixed / total).astype(jnp.bfloat16)


def first_kernel(pieces, rows, *refs):
    ins, outs = refs[:pieces], refs[pieces : 2 * pieces]
    queries, keys, values, results, sems, out_sems = refs[2 * pieces :]
    fetch = [
        pltpu.make_async_copy(
            ins[i].at[part], (queries, keys, values)[part].at[pl.ds(i * rows, rows)], sems.at[part, i]
        )
        for part in (1, 2, 0)
        for i in range(pieces)
    ]
    run_copies(fetch)

    @pl.loop(0, pieces)
    def _(i):
        here = pl.ds(pl.multiple_of(i * rows, rows), rows)
        results[here] = attend_block(queries[here], keys, values)

    run_copies(
        [
            pltpu.make_async_copy(results.at[pl.ds(i * rows, rows)], outs[i], out_sems.at[i])
            for i in range(pieces)
        ]
    )


def second_kernel(pieces, rows, count, flag, *refs):
    pairs, refs = refs[:pieces], refs[pieces:]
    queries_in, refs = refs[:count], refs[count:]
    earlier, refs = refs[:count], refs[count:]
    outs_a, outs_b = refs[:count], refs[count : 2 * count]
    queries, keys, values, results, sems, query_sems, a_sems, b_sems = refs[2 * count :]
    fetch = [
        pltpu.make_async_copy(
            pairs[i].at[part], (keys, values)[part].at[pl.ds(i * rows, rows)], sems.at[part, i]
        )
        for part in (0, 1)
        for i in range(pieces)
    ] + [
        pltpu.make_async_copy(queries_in[i], queries.at[pl.ds(i * rows, rows)], query_sems.at[i])
        for i in range(count)
    ]
    run_copies(fetch)

    @pl.loop(0, count)
    def _(i):
        here = pl.ds(pl.multiple_of(i * rows, rows), rows)
        results[here] = attend_block(queries[here], keys, values)

    @pl.when(flag[0] > 0)
    def _():
        run_copies([pltpu.make_async_copy(earlier[i], outs_a[i], a_sems.at[i]) for i in range(count)])

    @pl.when(flag[0] <= 0)
    def _():
        run_copies(
            [
                pltpu.make_async_copy(results.at[pl.ds(i * rows, rows)], outs_a[i], a_sems.at[i])
                for i in range(count)
            ]
        )

    run_copies(
        [
            pltpu.make_async_copy(results.at[pl.ds(i * rows, rows)], outs_b[i], b_sems.at[i])
            for i in range(count)
        ]
    )


def join_kernel(count, *refs):
    ins, out, sems = refs[:count], refs[count], refs[count + 1]
    run_copies([pltpu.make_async_copy(ins[i], out.at[i], sems.at[i]) for i in range(count)])


def final_kernel(pieces, order, flag, *refs):
    cached, refs = refs[0], refs[1:]
    from_a, refs = refs[:pieces], refs[pieces:]
    from_b, refs = refs[:pieces], refs[pieces:]
    far, out, sems = refs[:2], refs[2], refs[3]
    me = lax.axis_index("seq")
    half = pieces // 2

    @pl.when(flag[0] > 0)
    def _():
        copies = []
        for position, offset in enumerate(order):
            pieces_of = (from_a[offset], from_b[offset], far[position // half].at[position % half])
            for group, piece in enumerate(pieces_of):
                copies.append(
                    pltpu.make_async_copy(
                        piece,
                        out.at[0, :, head_columns(me, offset, group, pieces)],
                        sems.at[group, offset],
                    )
                )
        run_copies(copies)

    @pl.when(flag[0] <= 0)
    def _():
        run_copies([pltpu.make_async_copy(cached, out, sems.at[0, 0])])


def body(query_rows, key_rows, value_rows, cached_rows, plan, timestep, assignment):
    pieces = lax.axis_size("seq")
    slots = lax.axis_size("batch")
    rows = query_rows.shape[1]
    order = ring(pieces)
    kind = query_rows.dtype
    dma = pltpu.SemaphoreType.DMA

    def forward(value, offset):
        if offset == 0:
            return value
        return lax.ppermute(value, "seq", [(s, (s + offset) % pieces) for s in range(pieces)])

    def backward(value, offset):
        return forward(value, (pieces - offset) % pieces)

    def across(value):
        mask = slots // 2
        return lax.ppermute(value, "batch", [(s, s ^ mask) for s in range(slots)])

    def shape(*dims):
        return jax.ShapeDtypeStruct(dims, kind)

    sources = (query_rows, key_rows, value_rows)
    far_out, flag = pl.pallas_call(
        functools.partial(pack_far_kernel, pieces, 2),
        out_shape=(shape(pieces, 3, rows, HEAD_DIM), jax.ShapeDtypeStruct((1,), jnp.int32)),
        in_specs=[SMEM] * 3 + [ANY] * 3,
        out_specs=(ANY, SMEM),
        scratch_shapes=[dma((pieces, 3))],
        compiler_params=params(),
        name="pack_far",
    )(assignment, timestep, plan, *sources)
    first_out = pl.pallas_call(
        functools.partial(pack_kernel, pieces, 0),
        out_shape=[shape(3, rows, HEAD_DIM)] * pieces,
        in_specs=[ANY] * 3,
        out_specs=[ANY] * pieces,
        scratch_shapes=[dma((pieces, 3))],
        compiler_params=params(),
        name="pack_first",
    )(*sources)
    far_in = across(far_out)
    first_in = [None] * pieces
    for offset in order:
        first_in[offset] = forward(first_out[offset], offset)

    packed = pl.pallas_call(
        functools.partial(pack_second_kernel, pieces, 1),
        out_shape=[shape(2, rows, HEAD_DIM)] * pieces + [shape(rows, HEAD_DIM)] * pieces,
        in_specs=[SMEM] + [ANY] * 4,
        out_specs=[ANY] * (2 * pieces),
        scratch_shapes=[dma((pieces, 3))],
        compiler_params=params(),
        name="pack_second",
    )(flag, *sources, far_in)
    pairs_in = [None] * pieces
    queries_in = [None] * pieces
    for offset in order:
        pairs_in[offset] = forward(packed[offset], offset)
    for offset in order:
        queries_in[offset] = forward(packed[pieces + offset], offset)

    def cost(blocks):
        flops = blocks * rows * rows * pieces * HEAD_DIM * 4
        return pl.CostEstimate(
            flops=flops, bytes_accessed=2 * pieces * rows * HEAD_DIM * 2, transcendentals=blocks * rows * rows * pieces
        )

    first_result = pl.pallas_call(
        functools.partial(first_kernel, pieces, rows),
        out_shape=[shape(rows, HEAD_DIM)] * pieces,
        in_specs=[ANY] * pieces,
        out_specs=[ANY] * pieces,
        scratch_shapes=[pltpu.VMEM((pieces * rows, HEAD_DIM), kind)] * 4
        + [dma((3, pieces)), dma((pieces,))],
        compiler_params=params(),
        cost_estimate=cost(pieces),
        name="attend_first",
    )(*first_in)

    result_a = [None] * pieces
    result_b = [None] * pieces
    count = 2
    for begin in range(0, pieces, count):
        offsets = order[begin : begin + count]
        results = pl.pallas_call(
            functools.partial(second_kernel, pieces, rows, count),
            out_shape=[shape(rows, HEAD_DIM)] * (2 * count),
            in_specs=[SMEM] + [ANY] * (pieces + 2 * count),
            out_specs=[ANY] * (2 * count),
            scratch_shapes=[
                pltpu.VMEM((count * rows, HEAD_DIM), kind),
                pltpu.VMEM((pieces * rows, HEAD_DIM), kind),
                pltpu.VMEM((pieces * rows, HEAD_DIM), kind),
                pltpu.VMEM((count * rows, HEAD_DIM), kind),
                dma((2, pieces)),
                dma((count,)),
                dma((count,)),
                dma((count,)),
            ],
            compiler_params=params(),
            cost_estimate=cost(count),
            name=f"attend_second_{begin}",
        )(
            flag,
            *pairs_in,
            *[queries_in[offset] for offset in offsets],
            *[first_result[offset] for offset in offsets],
        )
        for i, offset in enumerate(offsets):
            result_a[offset] = results[i]
            result_b[offset] = results[count + i]

    back_a = [None] * pieces
    back_b = [None] * pieces
    for offset in order:
        back_a[offset] = backward(result_a[offset], offset)
    half = pieces // 2
    far_back = []
    for begin in range(0, pieces, half):
        joined = pl.pallas_call(
            functools.partial(join_kernel, half),
            out_shape=shape(half, rows, HEAD_DIM),
            in_specs=[ANY] * half,
            out_specs=ANY,
            scratch_shapes=[dma((half,))],
            compiler_params=params(),
            name=f"join_{begin}",
        )(*[back_a[offset] for offset in order[begin : begin + half]])
        far_back.append(across(joined))
    for offset in order:
        back_b[offset] = backward(result_b[offset], offset)

    return pl.pallas_call(
        functools.partial(final_kernel, pieces, order),
        out_shape=shape(*cached_rows.shape),
        in_specs=[SMEM] + [ANY] * (1 + 2 * pieces + 2),
        out_specs=ANY,
        scratch_shapes=[dma((GROUPS, pieces))],
        compiler_params=params(),
        name="final",
    )(flag, cached_rows, *back_a, *back_b, *far_back)


def solution(mesh):
    rows = P("batch", "seq", None)
    return jax.shard_map(
        body,
        mesh=mesh,
        in_specs=(rows, rows, rows, rows, P(), P(), P()),
        out_specs=rows,
        check_vma=False,
    )
```

```python
import functools
import math

import jax
import jax.numpy as jnp
from jax import lax
from jax.experimental import pallas as pl
from jax.experimental.pallas import tpu as pltpu
from jax.sharding import PartitionSpec as P

HEAD_DIM = 128
GROUPS = 3
SHARED = pltpu.CompilerParams(vmem_limit_bytes=40 << 20)

ANY = pl.BlockSpec(memory_space=pl.ANY)
HBM = pl.BlockSpec(memory_space=pltpu.HBM)
SMEM = pl.BlockSpec(memory_space=pltpu.SMEM)


def ring(pieces):
    order = [0]
    for step in range(1, pieces // 2):
        order += [step, pieces - step]
    if pieces > 1:
        order.append(pieces // 2)
    return order


def head_columns(me, offset, group, pieces):
    head = group * pieces + lax.rem(me + offset, pieces)
    return pl.ds(pl.multiple_of(head * HEAD_DIM, HEAD_DIM), HEAD_DIM)


def run_copies(copies):
    for copy in copies:
        copy.start()
    for copy in copies:
        copy.wait()


def pack_kernel(pieces, offsets, *refs):
    sources, outs, sems = refs[:3], refs[3:-1], refs[-1]
    me = lax.axis_index("seq")
    run_copies(
        [
            pltpu.make_async_copy(
                sources[part].at[0, :, head_columns(me, offset, 0, pieces)],
                outs[i].at[part],
                sems.at[i, part],
            )
            for i, offset in enumerate(offsets)
            for part in range(3)
        ]
    )


def pack_far_kernel(width, assignment, timestep, plan, *refs):
    sources, out, flag, sems = refs[:3], refs[3], refs[4], refs[5]
    copies = [
        pltpu.make_async_copy(
            sources[part].at[0, :, pl.ds((GROUPS - 1) * width, width)], out.at[part], sems.at[part]
        )
        for part in range(3)
    ]
    for copy in copies:
        copy.start()
    request = assignment[lax.axis_index("batch")]
    flag[0] = plan[request, timestep[request]]
    for copy in copies:
        copy.wait()


def pack_second_kernel(pieces, offsets, flag, *refs):
    sources, far = refs[:3], refs[3]
    outs, sems = refs[4:-1], refs[-1]
    me = lax.axis_index("seq")

    def move(own):
        run_copies(
            [
                pltpu.make_async_copy(
                    sources[part].at[0, :, head_columns(me, offset, 1, pieces)]
                    if own
                    else far.at[part, :, head_columns(me, offset, 0, pieces)],
                    outs[i].at[part],
                    sems.at[i, part],
                )
                for i, offset in enumerate(offsets)
                for part in range(3)
            ]
        )

    pl.when(flag[0] > 0)(lambda: move(True))
    pl.when(flag[0] <= 0)(lambda: move(False))


def attend(queries, keys, values, results, scores, block, looped):
    factor = math.log2(math.e) / math.sqrt(HEAD_DIM)
    total_keys = keys.shape[0]
    blocks = queries.shape[0] // block
    step = next(c for c in range(512, total_keys + 1, 128) if total_keys % c == 0)
    spans = [(begin, begin + step) for begin in range(0, total_keys, step)]

    def place(i):
        if isinstance(i, int):
            return pl.ds(i * block, block)
        return pl.ds(pl.multiple_of(i * block, block), block)

    def lanes(value):
        return [value[:, c : c + HEAD_DIM] for c in range(0, value.shape[1], HEAD_DIM)]

    def score(query, span, target, peak):
        part = lax.dot_general(
            query, keys[span[0] : span[1]], (((1,), (1,)), ((), ())), preferred_element_type=jnp.float32
        )
        target[:, span[0] : span[1]] = part
        return functools.reduce(jnp.maximum, lanes(part) + ([] if peak is None else [peak]))

    def weigh(source, span, top, total, mixed):
        shifted = jnp.exp2((source[:, span[0] : span[1]] - top) * factor)
        total = functools.reduce(jnp.add, lanes(shifted) + ([] if total is None else [total]))
        part = jnp.dot(
            shifted.astype(jnp.bfloat16), values[span[0] : span[1]], preferred_element_type=jnp.float32
        )
        return total, part if mixed is None else mixed + part

    def one(i, following, current, upcoming, top):
        peak = total = mixed = None
        if following is not None:
            query = queries[place(following)]
        for span in spans:
            if following is not None:
                peak = score(query, span, upcoming, peak)
            total, mixed = weigh(current, span, top, total, mixed)
        results[place(i)] = (mixed / jnp.sum(total, axis=1, keepdims=True)).astype(jnp.bfloat16)
        return None if following is None else jnp.max(peak, axis=1, keepdims=True)

    peak = None
    query = queries[place(0)]
    for span in spans:
        peak = score(query, span, scores[0], peak)
    top = jnp.max(peak, axis=1, keepdims=True)
    if looped:

        def pair(i, top):
            top = one(2 * i, 2 * i + 1, scores[0], scores[1], top)
            return one(2 * i + 1, jnp.minimum(2 * i + 2, blocks - 1), scores[1], scores[0], top)

        lax.fori_loop(0, blocks // 2, pair, top)
    else:
        for i in range(blocks):
            following = i + 1 if i + 1 < blocks else None
            top = one(i, following, scores[i % 2], scores[(i + 1) % 2], top)


def first_kernel(pieces, rows, *refs):
    ins, outs = refs[:pieces], refs[pieces : 2 * pieces]
    queries, keys, values, results, one_scores, other_scores, sems, out_sems = refs[2 * pieces :]
    run_copies(
        [
            pltpu.make_async_copy(
                ins[i].at[part], (queries, keys, values)[part].at[pl.ds(i * rows, rows)], sems.at[part, i]
            )
            for part in range(3)
            for i in range(pieces)
        ]
    )
    attend(queries, keys, values, results, (one_scores, other_scores), rows, True)
    run_copies(
        [
            pltpu.make_async_copy(results.at[pl.ds(i * rows, rows)], outs[i], out_sems.at[i])
            for i in range(pieces)
        ]
    )


def second_kernel(pieces, rows, offsets, *refs):
    count = len(offsets)
    ins, refs = refs[:pieces], refs[pieces:]
    earlier, outs, refs = refs[:count], refs[count : 2 * count], refs[2 * count :]
    queries, keys, values, results, one_scores, other_scores, sems, query_sems, out_sems = refs
    forwarded = [
        pltpu.make_async_copy(earlier[i], outs[i].at[0], out_sems.at[0, i]) for i in range(count)
    ]
    fetch = [
        pltpu.make_async_copy(
            ins[i].at[1 + part], (keys, values)[part].at[pl.ds(i * rows, rows)], sems.at[part, i]
        )
        for part in range(2)
        for i in range(pieces)
    ] + [
        pltpu.make_async_copy(ins[offset].at[0], queries.at[pl.ds(i * rows, rows)], query_sems.at[i])
        for i, offset in enumerate(offsets)
    ]
    for copy in forwarded:
        copy.start()
    run_copies(fetch)
    attend(queries, keys, values, results, (one_scores, other_scores), rows, False)
    run_copies(
        [
            pltpu.make_async_copy(results.at[pl.ds(i * rows, rows)], outs[i].at[1], out_sems.at[1, i])
            for i in range(count)
        ]
    )
    for copy in forwarded:
        copy.wait()


def join_kernel(count, *refs):
    ins, out, sems = refs[:count], refs[count], refs[count + 1]
    run_copies([pltpu.make_async_copy(ins[i].at[1], out.at[i], sems.at[i]) for i in range(count)])


def final_kernel(pieces, chunks, flag, *refs):
    cached, back = refs[0], refs[1 : 1 + pieces]
    far, out, sems = refs[1 + pieces : 1 + pieces + len(chunks)], refs[-2], refs[-1]
    me = lax.axis_index("seq")

    @pl.when(flag[0] > 0)
    def _():
        copies = []
        for chunk, offsets in enumerate(chunks):
            for i, offset in enumerate(offsets):
                for group, piece in enumerate(
                    (back[offset].at[0], back[offset].at[1], far[chunk].at[i])
                ):
                    copies.append(
                        pltpu.make_async_copy(
                            piece,
                            out.at[0, :, head_columns(me, offset, group, pieces)],
                            sems.at[group, offset],
                        )
                    )
        run_copies(copies)

    @pl.when(flag[0] <= 0)
    def _():
        run_copies([pltpu.make_async_copy(cached, out, sems.at[0, 0])])


def body(query_rows, key_rows, value_rows, cached_rows, plan, timestep, assignment):
    pieces = lax.axis_size("seq")
    slots = lax.axis_size("batch")
    rows = query_rows.shape[1]
    group_width = pieces * HEAD_DIM
    order = ring(pieces)
    kind = query_rows.dtype
    dma = pltpu.SemaphoreType.DMA
    sources = (query_rows, key_rows, value_rows)

    def forward(value, offset):
        if offset == 0:
            return value
        return lax.ppermute(value, "seq", [(s, (s + offset) % pieces) for s in range(pieces)])

    def backward(value, offset):
        return forward(value, (pieces - offset) % pieces)

    def across(value):
        mask = slots // 2
        return lax.ppermute(value, "batch", [(s, s ^ mask) for s in range(slots)])

    def shape(*dims):
        return jax.ShapeDtypeStruct(dims, kind)

    def cost(blocks):
        pairs = blocks * rows * rows * pieces
        return pl.CostEstimate(
            flops=pairs * HEAD_DIM * 4,
            bytes_accessed=(2 * pieces + 2 * blocks) * rows * HEAD_DIM * 2,
            transcendentals=pairs,
        )

    far_out, flag = pl.pallas_call(
        functools.partial(pack_far_kernel, group_width),
        out_shape=(shape(3, rows, group_width), jax.ShapeDtypeStruct((1,), jnp.int32)),
        in_specs=[SMEM] * 3 + [HBM] * 3,
        out_specs=(ANY, SMEM),
        scratch_shapes=[dma((3,))],
        name="pack_far",
    )(assignment, timestep, plan, *sources)
    far_in = across(far_out)

    def ordered(values, after):
        return lax.optimization_barrier((*values, after))[: len(values)]

    def pack_first(offsets, sources):
        return pl.pallas_call(
            functools.partial(pack_kernel, pieces, offsets),
            out_shape=[shape(3, rows, HEAD_DIM)] * len(offsets),
            in_specs=[HBM] * 3,
            out_specs=[ANY] * len(offsets),
            scratch_shapes=[dma((len(offsets), 3))],
            name="pack_first",
        )(*sources)

    def pack_second(offsets, sources):
        return pl.pallas_call(
            functools.partial(pack_second_kernel, pieces, offsets),
            out_shape=[shape(3, rows, HEAD_DIM)] * len(offsets),
            in_specs=[SMEM] + [HBM] * 3 + [ANY],
            out_specs=[ANY] * len(offsets),
            scratch_shapes=[dma((len(offsets), 3))],
            compiler_params=SHARED,
            name="pack_second",
        )(flag, *sources, far_in)

    first_in = [None] * pieces
    early, late = order[:5], order[5:]
    for offset, value in zip(early, pack_first(early, sources)):
        first_in[offset] = forward(value, offset)
    for i, offset in enumerate(late):
        (value,) = pack_first([offset], ordered(sources, first_in[order[1 + i]]))
        first_in[offset] = forward(value, offset)

    second_in = [None] * pieces
    early, late = order[:-1], order[-1:]
    for offset, value in zip(early, pack_second(early, sources)):
        second_in[offset] = forward(value, offset)

    first_result = pl.pallas_call(
        functools.partial(first_kernel, pieces, rows),
        out_shape=[shape(rows, HEAD_DIM)] * pieces,
        in_specs=[ANY] * pieces,
        out_specs=[ANY] * pieces,
        scratch_shapes=[pltpu.VMEM((pieces * rows, HEAD_DIM), kind)] * 4
        + [pltpu.VMEM((rows, pieces * rows), jnp.float32)] * 2
        + [dma((3, pieces)), dma((pieces,))],
        cost_estimate=cost(pieces),
        compiler_params=SHARED,
        name="attend_first",
    )(*ordered(first_in, second_in[order[1]]))

    for offset, value in zip(late, pack_second(late, ordered(sources, first_result[0]))):
        second_in[offset] = forward(value, offset)

    count = 2
    chunks = [order[begin : begin + count] for begin in range(0, pieces, count)]
    back = [None] * pieces
    for offsets in chunks:
        results = pl.pallas_call(
            functools.partial(second_kernel, pieces, rows, offsets),
            out_shape=[shape(2, rows, HEAD_DIM)] * count,
            in_specs=[ANY] * (pieces + count),
            out_specs=[ANY] * count,
            scratch_shapes=[
                pltpu.VMEM((count * rows, HEAD_DIM), kind),
                pltpu.VMEM((pieces * rows, HEAD_DIM), kind),
                pltpu.VMEM((pieces * rows, HEAD_DIM), kind),
                pltpu.VMEM((count * rows, HEAD_DIM), kind),
                pltpu.VMEM((rows, pieces * rows), jnp.float32),
                pltpu.VMEM((rows, pieces * rows), jnp.float32),
                dma((2, pieces)),
                dma((count,)),
                dma((2, count)),
            ],
            cost_estimate=cost(count),
            compiler_params=SHARED,
            name="attend_second",
        )(*second_in, *[first_result[offset] for offset in offsets])
        for offset, value in zip(offsets, results):
            back[offset] = backward(value, offset)

    far_back = []
    for offsets in chunks:
        joined = pl.pallas_call(
            functools.partial(join_kernel, count),
            out_shape=shape(count, rows, HEAD_DIM),
            in_specs=[ANY] * count,
            out_specs=ANY,
            scratch_shapes=[dma((count,))],
            compiler_params=SHARED,
            name="join",
        )(*[back[offset] for offset in offsets])
        far_back.append(across(joined))

    return pl.pallas_call(
        functools.partial(final_kernel, pieces, chunks),
        out_shape=shape(*cached_rows.shape),
        in_specs=[SMEM, HBM] + [ANY] * (pieces + len(chunks)),
        out_specs=ANY,
        scratch_shapes=[dma((GROUPS, pieces))],
        compiler_params=SHARED,
        name="final",
    )(flag, cached_rows, *back, *far_back)


def solution(mesh):
    rows = P("batch", "seq", None)
    return jax.shard_map(
        body,
        mesh=mesh,
        in_specs=(rows, rows, rows, rows, P(), P(), P()),
        out_specs=rows,
        check_vma=False,
    )
```

```python
import functools
import math

import jax
import jax.numpy as jnp
from jax import lax
from jax.experimental import pallas as pl
from jax.experimental.pallas import tpu as pltpu
from jax.sharding import PartitionSpec as P

HEAD_DIM = 128
GROUPS = 3
SHARED = pltpu.CompilerParams(vmem_limit_bytes=40 << 20)

ANY = pl.BlockSpec(memory_space=pl.ANY)
HBM = pl.BlockSpec(memory_space=pltpu.HBM)
VMEM = pl.BlockSpec(memory_space=pltpu.VMEM)
SMEM = pl.BlockSpec(memory_space=pltpu.SMEM)


def ring(pieces):
    order = [0]
    for step in range(1, pieces // 2):
        order += [step, pieces - step]
    if pieces > 1:
        order.append(pieces // 2)
    return order


def head_columns(me, offset, group, pieces):
    head = group * pieces + lax.rem(me + offset, pieces)
    return pl.ds(pl.multiple_of(head * HEAD_DIM, HEAD_DIM), HEAD_DIM)


def run_copies(copies):
    for copy in copies:
        copy.start()
    for copy in copies:
        copy.wait()


def run_staged(pairs):
    for load, _ in pairs:
        load.start()
    for load, store in pairs:
        load.wait()
        store.start()
    for _, store in pairs:
        store.wait()


def pack_kernel(pieces, offsets, *refs):
    sources, outs, stage, sems, out_sems = refs[:3], refs[3:-3], refs[-3], refs[-2], refs[-1]
    me = lax.axis_index("seq")
    run_staged(
        [
            (
                pltpu.make_async_copy(
                    sources[part].at[0, :, head_columns(me, offset, 0, pieces)],
                    stage.at[i, part],
                    sems.at[i, part],
                ),
                pltpu.make_async_copy(stage.at[i, part], outs[i].at[part], out_sems.at[i, part]),
            )
            for i, offset in enumerate(offsets)
            for part in range(3)
        ]
    )


def pack_far_kernel(width, assignment, timestep, plan, *refs):
    sources, out, flag, stage, sems, out_sems = refs[:3], *refs[3:]
    request = assignment[lax.axis_index("batch")]
    flag[0] = plan[request, timestep[request]]
    run_staged(
        [
            (
                pltpu.make_async_copy(
                    sources[part].at[0, :, pl.ds((GROUPS - 1) * width, width)],
                    stage.at[part],
                    sems.at[part],
                ),
                pltpu.make_async_copy(stage.at[part], out.at[part], out_sems.at[part]),
            )
            for part in range(3)
        ]
    )


def pack_second_kernel(pieces, offsets, flag, *refs):
    sources, far = refs[:3], refs[3]
    outs, sems = refs[4:-1], refs[-1]
    me = lax.axis_index("seq")

    def move(own):
        run_copies(
            [
                pltpu.make_async_copy(
                    sources[part].at[0, :, head_columns(me, offset, 1, pieces)]
                    if own
                    else far.at[part, :, head_columns(me, offset, 0, pieces)],
                    outs[i].at[part],
                    sems.at[i, part],
                )
                for i, offset in enumerate(offsets)
                for part in range(3)
            ]
        )

    pl.when(flag[0] > 0)(lambda: move(True))
    pl.when(flag[0] <= 0)(lambda: move(False))


def attend(queries, keys, values, results, scores, block, looped):
    factor = math.log2(math.e) / math.sqrt(HEAD_DIM)
    total_keys = keys.shape[0]
    blocks = queries.shape[0] // block
    step = next(c for c in range(512, total_keys + 1, 128) if total_keys % c == 0)
    spans = [(begin, begin + step) for begin in range(0, total_keys, step)]

    def place(i):
        if isinstance(i, int):
            return pl.ds(i * block, block)
        return pl.ds(pl.multiple_of(i * block, block), block)

    def lanes(value):
        return [value[:, c : c + HEAD_DIM] for c in range(0, value.shape[1], HEAD_DIM)]

    def score(query, span, target, peak):
        part = lax.dot_general(
            query, keys[span[0] : span[1]], (((1,), (1,)), ((), ())), preferred_element_type=jnp.float32
        )
        target[:, span[0] : span[1]] = part
        return functools.reduce(jnp.maximum, lanes(part) + ([] if peak is None else [peak]))

    def weigh(source, span, top, total, mixed):
        shifted = jnp.exp2((source[:, span[0] : span[1]] - top) * factor)
        total = functools.reduce(jnp.add, lanes(shifted) + ([] if total is None else [total]))
        part = jnp.dot(
            shifted.astype(jnp.bfloat16), values[span[0] : span[1]], preferred_element_type=jnp.float32
        )
        return total, part if mixed is None else mixed + part

    def one(i, following, current, upcoming, top):
        peak = total = mixed = None
        if following is not None:
            query = queries[place(following)]
        for span in spans:
            if following is not None:
                peak = score(query, span, upcoming, peak)
            total, mixed = weigh(current, span, top, total, mixed)
        results[place(i)] = (mixed / jnp.sum(total, axis=1, keepdims=True)).astype(jnp.bfloat16)
        return None if following is None else jnp.max(peak, axis=1, keepdims=True)

    peak = None
    query = queries[place(0)]
    for span in spans:
        peak = score(query, span, scores[0], peak)
    top = jnp.max(peak, axis=1, keepdims=True)
    if looped:

        def pair(i, top):
            top = one(2 * i, 2 * i + 1, scores[0], scores[1], top)
            return one(2 * i + 1, jnp.minimum(2 * i + 2, blocks - 1), scores[1], scores[0], top)

        lax.fori_loop(0, blocks // 2, pair, top)
    else:
        for i in range(blocks):
            following = i + 1 if i + 1 < blocks else None
            top = one(i, following, scores[i % 2], scores[(i + 1) % 2], top)


def gather_rows(ins, rows, part, target):
    for i, piece in enumerate(ins):
        target[i * rows : (i + 1) * rows] = piece[part]


def first_kernel(pieces, rows, *refs):
    ins, results = refs[:pieces], refs[pieces]
    queries, keys, values, one_scores, other_scores = refs[pieces + 1 :]
    for part, target in enumerate((queries, keys, values)):
        gather_rows(ins, rows, part, target)
    attend(queries, keys, values, results, (one_scores, other_scores), rows, True)


def second_kernel(pieces, rows, positions, *refs):
    count = len(positions)
    ins, earlier, outs = refs[:pieces], refs[pieces], refs[pieces + 1 : pieces + 1 + count]
    queries, keys, values, results, one_scores, other_scores = refs[pieces + 1 + count :]
    gather_rows(ins, rows, 1, keys)
    gather_rows(ins, rows, 2, values)
    gather_rows([ins[p] for p in positions], rows, 0, queries)
    attend(queries, keys, values, results, (one_scores, other_scores), rows, False)
    for i, position in enumerate(positions):
        outs[i][0] = earlier[position * rows : (position + 1) * rows]
        outs[i][1] = results[i * rows : (i + 1) * rows]


def join_kernel(count, *refs):
    for i in range(count):
        refs[count][i] = refs[i][1]


def final_kernel(pieces, chunks, flag, *refs):
    cached, back = refs[0], refs[1 : 1 + pieces]
    far, out, sems = refs[1 + pieces : 1 + pieces + len(chunks)], refs[-2], refs[-1]
    me = lax.axis_index("seq")

    @pl.when(flag[0] > 0)
    def _():
        copies = []
        for chunk, offsets in enumerate(chunks):
            for i, offset in enumerate(offsets):
                for group, piece in enumerate(
                    (back[offset].at[0], back[offset].at[1], far[chunk].at[i])
                ):
                    copies.append(
                        pltpu.make_async_copy(
                            piece,
                            out.at[0, :, head_columns(me, offset, group, pieces)],
                            sems.at[group, offset],
                        )
                    )
        run_copies(copies)

    @pl.when(flag[0] <= 0)
    def _():
        run_copies([pltpu.make_async_copy(cached, out, sems.at[0, 0])])


def body(query_rows, key_rows, value_rows, cached_rows, plan, timestep, assignment):
    pieces = lax.axis_size("seq")
    slots = lax.axis_size("batch")
    rows = query_rows.shape[1]
    group_width = pieces * HEAD_DIM
    order = ring(pieces)
    kind = query_rows.dtype
    dma = pltpu.SemaphoreType.DMA
    sources = (query_rows, key_rows, value_rows)

    def forward(value, offset):
        if offset == 0:
            return value
        return lax.ppermute(value, "seq", [(s, (s + offset) % pieces) for s in range(pieces)])

    def backward(value, offset):
        return forward(value, (pieces - offset) % pieces)

    def across(value):
        mask = slots // 2
        return lax.ppermute(value, "batch", [(s, s ^ mask) for s in range(slots)])

    def shape(*dims):
        return jax.ShapeDtypeStruct(dims, kind)

    def cost(blocks):
        pairs = blocks * rows * rows * pieces
        return pl.CostEstimate(
            flops=pairs * HEAD_DIM * 4,
            bytes_accessed=(2 * pieces + 2 * blocks) * rows * HEAD_DIM * 2,
            transcendentals=pairs,
        )

    far_out, flag = pl.pallas_call(
        functools.partial(pack_far_kernel, group_width),
        out_shape=(shape(3, rows, group_width), jax.ShapeDtypeStruct((1,), jnp.int32)),
        in_specs=[SMEM] * 3 + [HBM] * 3,
        out_specs=(ANY, SMEM),
        scratch_shapes=[pltpu.VMEM((3, rows, group_width), kind), dma((3,)), dma((3,))],
        name="pack_far",
    )(assignment, timestep, plan, *sources)
    far_in = across(far_out)

    def ordered(values, after):
        return lax.optimization_barrier((*values, after))[: len(values)]

    def pack_first(offsets, sources):
        return pl.pallas_call(
            functools.partial(pack_kernel, pieces, offsets),
            out_shape=[shape(3, rows, HEAD_DIM)] * len(offsets),
            in_specs=[HBM] * 3,
            out_specs=[ANY] * len(offsets),
            scratch_shapes=[
                pltpu.VMEM((len(offsets), 3, rows, HEAD_DIM), kind),
                dma((len(offsets), 3)),
                dma((len(offsets), 3)),
            ],
            name="pack_first",
        )(*sources)

    def pack_second(offsets, sources):
        return pl.pallas_call(
            functools.partial(pack_second_kernel, pieces, offsets),
            out_shape=[shape(3, rows, HEAD_DIM)] * len(offsets),
            in_specs=[SMEM] + [HBM] * 3 + [ANY],
            out_specs=[ANY] * len(offsets),
            scratch_shapes=[dma((len(offsets), 3))],
            compiler_params=SHARED,
            name="pack_second",
        )(flag, *sources, far_in)

    first_in = [None] * pieces
    early, late = order[:5], order[5:]
    for offset, value in zip(early, pack_first(early, sources)):
        first_in[offset] = forward(value, offset)
    for i, offset in enumerate(late):
        (value,) = pack_first([offset], ordered(sources, first_in[order[1 + i]]))
        first_in[offset] = forward(value, offset)

    second_in = [None] * pieces
    early, late = order[:-1], order[-1:]
    for offset, value in zip(early, pack_second(early, sources)):
        second_in[offset] = forward(value, offset)

    score_buffers = [pltpu.VMEM((rows, pieces * rows), jnp.float32)] * 2
    first_result = pl.pallas_call(
        functools.partial(first_kernel, pieces, rows),
        out_shape=shape(pieces * rows, HEAD_DIM),
        in_specs=[VMEM] * pieces,
        out_specs=VMEM,
        scratch_shapes=[pltpu.VMEM((pieces * rows, HEAD_DIM), kind)] * 3 + score_buffers,
        compiler_params=SHARED,
        cost_estimate=cost(pieces),
        name="attend_first",
    )(*ordered(first_in, second_in[order[1]]))

    for offset, value in zip(late, pack_second(late, ordered(sources, first_result))):
        second_in[offset] = forward(value, offset)

    count = 2
    chunks = [order[begin : begin + count] for begin in range(0, pieces, count)]
    back = [None] * pieces
    for offsets in chunks:
        results = pl.pallas_call(
            functools.partial(second_kernel, pieces, rows, offsets),
            out_shape=[shape(2, rows, HEAD_DIM)] * count,
            in_specs=[VMEM] * (pieces + 1),
            out_specs=[VMEM] * count,
            scratch_shapes=[
                pltpu.VMEM((count * rows, HEAD_DIM), kind),
                pltpu.VMEM((pieces * rows, HEAD_DIM), kind),
                pltpu.VMEM((pieces * rows, HEAD_DIM), kind),
                pltpu.VMEM((count * rows, HEAD_DIM), kind),
                *score_buffers,
            ],
            compiler_params=SHARED,
            cost_estimate=cost(count),
            name="attend_second",
        )(*second_in, first_result)
        for offset, value in zip(offsets, results):
            back[offset] = backward(value, offset)

    far_back = []
    for offsets in chunks:
        joined = pl.pallas_call(
            functools.partial(join_kernel, count),
            out_shape=shape(count, rows, HEAD_DIM),
            in_specs=[VMEM] * count,
            out_specs=VMEM,
            compiler_params=SHARED,
            name="join",
        )(*[back[offset] for offset in offsets])
        far_back.append(across(joined))

    return pl.pallas_call(
        functools.partial(final_kernel, pieces, chunks),
        out_shape=shape(*cached_rows.shape),
        in_specs=[SMEM, HBM] + [ANY] * (pieces + len(chunks)),
        out_specs=ANY,
        scratch_shapes=[dma((GROUPS, pieces))],
        compiler_params=SHARED,
        name="final",
    )(flag, cached_rows, *back, *far_back)


def solution(mesh):
    rows = P("batch", "seq", None)
    return jax.shard_map(
        body,
        mesh=mesh,
        in_specs=(rows, rows, rows, rows, P(), P(), P()),
        out_specs=rows,
        check_vma=False,
    )
```

```python
import functools
import math

import jax
import jax.numpy as jnp
from jax import lax
from jax.experimental import pallas as pl
from jax.experimental.pallas import tpu as pltpu
from jax.sharding import PartitionSpec as P

HEAD_DIM = 128
GROUPS = 3
PACK = pltpu.CompilerParams(vmem_limit_bytes=48 << 20)
SHARED = pltpu.CompilerParams(vmem_limit_bytes=40 << 20)

ANY = pl.BlockSpec(memory_space=pl.ANY)
HBM = pl.BlockSpec(memory_space=pltpu.HBM)
VMEM = pl.BlockSpec(memory_space=pltpu.VMEM)
SMEM = pl.BlockSpec(memory_space=pltpu.SMEM)


def ring(pieces):
    half = pieces // 2
    return [step for near in range(1, half) for step in (near, pieces - near)] + [half]


def head_columns(me, offset, group, pieces):
    head = group * pieces + lax.rem(me + offset, pieces)
    return pl.ds(pl.multiple_of(head * HEAD_DIM, HEAD_DIM), HEAD_DIM)


def run_copies(copies):
    for copy in copies:
        copy.start()
    for copy in copies:
        copy.wait()


def pack_kernel(pieces, offsets, *refs):
    sources, outs, sems = refs[:3], refs[3:-1], refs[-1]
    me = lax.axis_index("seq")
    run_copies(
        [
            pltpu.make_async_copy(
                sources[part].at[0, :, head_columns(me, offset, 0, pieces)],
                outs[i].at[part],
                sems.at[i, part],
            )
            for i, offset in enumerate(offsets)
            for part in range(3)
        ]
    )


def pack_far_kernel(width, *refs):
    sources, out, sems = refs[:3], refs[3], refs[4]
    run_copies(
        [
            pltpu.make_async_copy(
                sources[part].at[0, :, pl.ds((GROUPS - 1) * width, width)], out.at[part], sems.at[part]
            )
            for part in range(3)
        ]
    )


def flag_kernel(assignment, timestep, plan, flag):
    request = assignment[lax.axis_index("batch")]
    flag[0] = plan[request, timestep[request]]


def pack_second_kernel(pieces, offsets, flag, *refs):
    sources, far = refs[:3], refs[3]
    outs, sems = refs[4:-1], refs[-1]
    me = lax.axis_index("seq")

    def move(own):
        run_copies(
            [
                pltpu.make_async_copy(
                    sources[part].at[0, :, head_columns(me, offset, 1, pieces)]
                    if own
                    else far.at[part, :, head_columns(me, offset, 0, pieces)],
                    outs[i].at[part],
                    sems.at[i, part],
                )
                for i, offset in enumerate(offsets)
                for part in range(3)
            ]
        )

    pl.when(flag[0] > 0)(lambda: move(True))
    pl.when(flag[0] <= 0)(lambda: move(False))


def attend(queries, keys, values, results, scores, block, looped):
    factor = math.log2(math.e) / math.sqrt(HEAD_DIM)
    total_keys = keys.shape[0]
    blocks = queries.shape[0] // block
    step = next(c for c in range(512, total_keys + 1, 128) if total_keys % c == 0)
    spans = [(begin, begin + step) for begin in range(0, total_keys, step)]

    def place(i):
        if isinstance(i, int):
            return pl.ds(i * block, block)
        return pl.ds(pl.multiple_of(i * block, block), block)

    def lanes(value):
        return [value[:, c : c + HEAD_DIM] for c in range(0, value.shape[1], HEAD_DIM)]

    def score(query, span, target, peak):
        part = lax.dot_general(
            query, keys[span[0] : span[1]], (((1,), (1,)), ((), ())), preferred_element_type=jnp.float32
        )
        target[:, span[0] : span[1]] = part
        return functools.reduce(jnp.maximum, lanes(part) + ([] if peak is None else [peak]))

    def weigh(source, span, top, total, mixed):
        shifted = jnp.exp2((source[:, span[0] : span[1]] - top) * factor)
        total = functools.reduce(jnp.add, lanes(shifted) + ([] if total is None else [total]))
        part = jnp.dot(
            shifted.astype(jnp.bfloat16), values[span[0] : span[1]], preferred_element_type=jnp.float32
        )
        return total, part if mixed is None else mixed + part

    def one(i, following, current, upcoming, top):
        peak = total = mixed = None
        if following is not None:
            query = queries[place(following)]
        for span in spans:
            if following is not None:
                peak = score(query, span, upcoming, peak)
            total, mixed = weigh(current, span, top, total, mixed)
        results[place(i)] = (mixed / jnp.sum(total, axis=1, keepdims=True)).astype(jnp.bfloat16)
        return None if following is None else jnp.max(peak, axis=1, keepdims=True)

    peak = None
    query = queries[place(0)]
    for span in spans:
        peak = score(query, span, scores[0], peak)
    top = jnp.max(peak, axis=1, keepdims=True)
    if looped:

        def pair(i, top):
            top = one(2 * i, 2 * i + 1, scores[0], scores[1], top)
            return one(2 * i + 1, jnp.minimum(2 * i + 2, blocks - 1), scores[1], scores[0], top)

        lax.fori_loop(0, blocks // 2, pair, top)
    else:
        for i in range(blocks):
            following = i + 1 if i + 1 < blocks else None
            top = one(i, following, scores[i % 2], scores[(i + 1) % 2], top)


def gather_rows(ins, rows, part, target):
    for i, piece in enumerate(ins):
        target[i * rows : (i + 1) * rows] = piece[part]


def first_kernel(pieces, rows, *refs):
    ins, results = refs[:pieces], refs[pieces]
    queries, keys, values, one_scores, other_scores = refs[pieces + 1 :]
    for part, target in enumerate((queries, keys, values)):
        gather_rows(ins, rows, part, target)
    attend(queries, keys, values, results, (one_scores, other_scores), rows, True)


def second_kernel(pieces, rows, positions, *refs):
    count = len(positions)
    ins, earlier, outs = refs[:pieces], refs[pieces], refs[pieces + 1 : pieces + 1 + count]
    queries, keys, values, results, one_scores, other_scores = refs[pieces + 1 + count :]
    gather_rows(ins, rows, 1, keys)
    gather_rows(ins, rows, 2, values)
    gather_rows([ins[p] for p in positions], rows, 0, queries)
    attend(queries, keys, values, results, (one_scores, other_scores), rows, False)
    for i, position in enumerate(positions):
        outs[i][0] = earlier[position * rows : (position + 1) * rows]
        outs[i][1] = results[i * rows : (i + 1) * rows]


def join_kernel(*refs):
    for i, piece in enumerate(refs[:-1]):
        refs[-1][i] = piece[1]


def final_kernel(pieces, joins, flag, *refs):
    cached, back = refs[0], refs[1 : 1 + pieces]
    far, out, sems = refs[1 + pieces : 1 + pieces + len(joins)], refs[-2], refs[-1]
    me = lax.axis_index("seq")

    @pl.when(flag[0] > 0)
    def _():
        copies = []
        for join, offsets in enumerate(joins):
            for i, offset in enumerate(offsets):
                for group, piece in enumerate(
                    (back[offset].at[0], back[offset].at[1], far[join].at[i])
                ):
                    copies.append(
                        pltpu.make_async_copy(
                            piece,
                            out.at[0, :, head_columns(me, offset, group, pieces)],
                            sems.at[group, offset],
                        )
                    )
        run_copies(copies)

    @pl.when(flag[0] <= 0)
    def _():
        run_copies([pltpu.make_async_copy(cached, out, sems.at[0, 0])])


def body(query_rows, key_rows, value_rows, cached_rows, plan, timestep, assignment):
    pieces = lax.axis_size("seq")
    slots = lax.axis_size("batch")
    rows = query_rows.shape[1]
    group_width = pieces * HEAD_DIM
    order = ring(pieces)
    kind = query_rows.dtype
    dma = pltpu.SemaphoreType.DMA
    sources = (query_rows, key_rows, value_rows)

    def forward(value, offset):
        if offset == 0:
            return value
        return lax.ppermute(value, "seq", [(s, (s + offset) % pieces) for s in range(pieces)])

    def backward(value, offset):
        return forward(value, (pieces - offset) % pieces)

    def across(value):
        mask = slots // 2
        return lax.ppermute(value, "batch", [(s, s ^ mask) for s in range(slots)])

    def shape(*dims):
        return jax.ShapeDtypeStruct(dims, kind)

    def cost(blocks):
        pairs = blocks * rows * rows * pieces
        return pl.CostEstimate(
            flops=pairs * HEAD_DIM * 4,
            bytes_accessed=(2 * pieces + 2 * blocks) * rows * HEAD_DIM * 2,
            transcendentals=pairs,
        )

    far_out = pl.pallas_call(
        functools.partial(pack_far_kernel, group_width),
        out_shape=shape(3, rows, group_width),
        in_specs=[HBM] * 3,
        out_specs=VMEM,
        scratch_shapes=[dma((3,))],
        name="pack_far",
    )(*sources)
    far_in = across(far_out)

    def ordered(values, after):
        return lax.optimization_barrier((*values, after))[: len(values)]

    def pack_first(offsets, sources):
        return pl.pallas_call(
            functools.partial(pack_kernel, pieces, offsets),
            out_shape=[shape(3, rows, HEAD_DIM)] * len(offsets),
            in_specs=[HBM] * 3,
            out_specs=[VMEM] * len(offsets),
            scratch_shapes=[dma((len(offsets), 3))],
            name="pack_first",
        )(*sources)

    def pack_second(offsets, sources):
        return pl.pallas_call(
            functools.partial(pack_second_kernel, pieces, offsets),
            out_shape=[shape(3, rows, HEAD_DIM)] * len(offsets),
            in_specs=[SMEM] + [HBM] * 3 + [ANY],
            out_specs=[VMEM] * len(offsets),
            scratch_shapes=[dma((len(offsets), 3))],
            compiler_params=PACK,
            name="pack_second",
        )(flag, *sources, far_in)

    first_in = [None] * pieces
    for offsets, awaited in (([*order[:4], 0], None), ([order[4]], order[0]), ([order[5]], order[1]), ([order[6]], order[2])):
        values = sources if awaited is None else ordered(sources, first_in[awaited])
        for offset, value in zip(offsets, pack_first(offsets, values)):
            first_in[offset] = forward(value, offset)

    flag = pl.pallas_call(
        flag_kernel,
        out_shape=jax.ShapeDtypeStruct((1,), jnp.int32),
        in_specs=[SMEM] * 3,
        out_specs=SMEM,
        name="flag",
    )(*ordered((assignment, timestep, plan), first_in[order[2]]))

    second_in = [None] * pieces
    early, late = [*order[:-1], 0], order[-1:]
    for offset, value in zip(early, pack_second(early, sources)):
        second_in[offset] = forward(value, offset)

    score_buffers = [pltpu.VMEM((rows, pieces * rows), jnp.float32)] * 2
    first_result = pl.pallas_call(
        functools.partial(first_kernel, pieces, rows),
        out_shape=shape(pieces * rows, HEAD_DIM),
        in_specs=[VMEM] * pieces,
        out_specs=VMEM,
        scratch_shapes=[pltpu.VMEM((pieces * rows, HEAD_DIM), kind)] * 3 + score_buffers,
        compiler_params=SHARED,
        cost_estimate=cost(pieces),
        name="attend_first",
    )(*ordered(first_in, second_in[order[0]]))

    for offset, value in zip(late, pack_second(late, ordered(sources, first_result))):
        second_in[offset] = forward(value, offset)

    count = 2
    sends = [order[6], order[4], order[5], *order[2:4], *order[:2], 0]
    chunks = [sends[begin : begin + count] for begin in range(0, pieces, count)]
    back = [None] * pieces
    for offsets in chunks:
        results = pl.pallas_call(
            functools.partial(second_kernel, pieces, rows, offsets),
            out_shape=[shape(2, rows, HEAD_DIM)] * count,
            in_specs=[VMEM] * (pieces + 1),
            out_specs=[VMEM] * count,
            scratch_shapes=[
                pltpu.VMEM((count * rows, HEAD_DIM), kind),
                pltpu.VMEM((pieces * rows, HEAD_DIM), kind),
                pltpu.VMEM((pieces * rows, HEAD_DIM), kind),
                pltpu.VMEM((count * rows, HEAD_DIM), kind),
                *score_buffers,
            ],
            compiler_params=SHARED,
            cost_estimate=cost(count),
            name="attend_second",
        )(*second_in, first_result)
        for offset, value in zip(offsets, results):
            back[offset] = backward(value, offset)

    joins = [chunks[0] + chunks[1], *chunks[2:]]
    far_back = []
    for offsets in joins:
        joined = pl.pallas_call(
            join_kernel,
            out_shape=shape(len(offsets), rows, HEAD_DIM),
            in_specs=[VMEM] * len(offsets),
            out_specs=VMEM,
            compiler_params=SHARED,
            name="join",
        )(*[back[offset] for offset in offsets])
        far_back.append(across(joined))

    return pl.pallas_call(
        functools.partial(final_kernel, pieces, joins),
        out_shape=shape(*cached_rows.shape),
        in_specs=[SMEM, HBM] + [ANY] * (pieces + len(joins)),
        out_specs=ANY,
        scratch_shapes=[dma((GROUPS, pieces))],
        compiler_params=SHARED,
        name="final",
    )(flag, cached_rows, *back, *far_back)


def solution(mesh):
    rows = P("batch", "seq", None)
    return jax.shard_map(
        body,
        mesh=mesh,
        in_specs=(rows, rows, rows, rows, P(), P(), P()),
        out_specs=rows,
        check_vma=False,
    )
```

```python
import functools
import math

import jax
import jax.numpy as jnp
from jax import lax
from jax.experimental import pallas as pl
from jax.experimental.pallas import tpu as pltpu
from jax.sharding import PartitionSpec as P

HEAD_DIM = 128
GROUPS = 3
PACK = pltpu.CompilerParams(vmem_limit_bytes=48 << 20)
SHARED = pltpu.CompilerParams(vmem_limit_bytes=40 << 20)

ANY = pl.BlockSpec(memory_space=pl.ANY)
HBM = pl.BlockSpec(memory_space=pltpu.HBM)
VMEM = pl.BlockSpec(memory_space=pltpu.VMEM)
SMEM = pl.BlockSpec(memory_space=pltpu.SMEM)


def ring(pieces):
    half = pieces // 2
    return [step for near in range(1, half) for step in (near, pieces - near)] + [half]


def head_columns(me, offset, group, pieces):
    head = group * pieces + lax.rem(me + offset, pieces)
    return pl.ds(pl.multiple_of(head * HEAD_DIM, HEAD_DIM), HEAD_DIM)


def run_copies(copies):
    for copy in copies:
        copy.start()
    for copy in copies:
        copy.wait()


def pack_kernel(pieces, offsets, *refs):
    sources, outs, sems = refs[:3], refs[3:-1], refs[-1]
    me = lax.axis_index("seq")
    run_copies(
        [
            pltpu.make_async_copy(
                sources[part].at[0, :, head_columns(me, offset, 0, pieces)],
                outs[i].at[part],
                sems.at[i, part],
            )
            for i, offset in enumerate(offsets)
            for part in range(3)
        ]
    )


def pack_far_kernel(width, *refs):
    sources, out, sems = refs[:3], refs[3], refs[4]
    run_copies(
        [
            pltpu.make_async_copy(
                sources[part].at[0, :, pl.ds((GROUPS - 1) * width, width)], out.at[part], sems.at[part]
            )
            for part in range(3)
        ]
    )


def flag_kernel(assignment, timestep, plan, flag):
    request = assignment[lax.axis_index("batch")]
    flag[0] = plan[request, timestep[request]]


def pack_second_kernel(pieces, offsets, flag, *refs):
    sources, far = refs[:3], refs[3]
    outs, sems = refs[4:-1], refs[-1]
    me = lax.axis_index("seq")

    def move(own):
        run_copies(
            [
                pltpu.make_async_copy(
                    sources[part].at[0, :, head_columns(me, offset, 1, pieces)]
                    if own
                    else far.at[part, :, head_columns(me, offset, 0, pieces)],
                    outs[i].at[part],
                    sems.at[i, part],
                )
                for i, offset in enumerate(offsets)
                for part in range(3)
            ]
        )

    pl.when(flag[0] > 0)(lambda: move(True))
    pl.when(flag[0] <= 0)(lambda: move(False))


def attend(queries, keys, values, results, scores, block, looped):
    factor = math.log2(math.e) / math.sqrt(HEAD_DIM)
    total_keys = keys.shape[0]
    blocks = queries.shape[0] // block
    step = next(c for c in range(512, total_keys + 1, 128) if total_keys % c == 0)
    spans = [(begin, begin + step) for begin in range(0, total_keys, step)]

    def place(i):
        if isinstance(i, int):
            return pl.ds(i * block, block)
        return pl.ds(pl.multiple_of(i * block, block), block)

    def lanes(value):
        return [value[:, c : c + HEAD_DIM] for c in range(0, value.shape[1], HEAD_DIM)]

    def score(query, span, target, peak):
        part = lax.dot_general(
            query, keys[span[0] : span[1]], (((1,), (1,)), ((), ())), preferred_element_type=jnp.float32
        )
        target[:, span[0] : span[1]] = part
        return functools.reduce(jnp.maximum, lanes(part) + ([] if peak is None else [peak]))

    def weigh(source, span, top, total, mixed):
        shifted = jnp.exp2((source[:, span[0] : span[1]] - top) * factor)
        total = functools.reduce(jnp.add, lanes(shifted) + ([] if total is None else [total]))
        part = jnp.dot(
            shifted.astype(jnp.bfloat16), values[span[0] : span[1]], preferred_element_type=jnp.float32
        )
        return total, part if mixed is None else mixed + part

    def one(i, following, current, upcoming, top):
        peak = total = mixed = None
        if following is not None:
            query = queries[place(following)]
        for span in spans:
            if following is not None:
                peak = score(query, span, upcoming, peak)
            total, mixed = weigh(current, span, top, total, mixed)
        results[place(i)] = (mixed / jnp.sum(total, axis=1, keepdims=True)).astype(jnp.bfloat16)
        return None if following is None else jnp.max(peak, axis=1, keepdims=True)

    peak = None
    query = queries[place(0)]
    for span in spans:
        peak = score(query, span, scores[0], peak)
    top = jnp.max(peak, axis=1, keepdims=True)
    if looped:

        def pair(i, top):
            top = one(2 * i, 2 * i + 1, scores[0], scores[1], top)
            return one(2 * i + 1, jnp.minimum(2 * i + 2, blocks - 1), scores[1], scores[0], top)

        lax.fori_loop(0, blocks // 2, pair, top)
    else:
        for i in range(blocks):
            following = i + 1 if i + 1 < blocks else None
            top = one(i, following, scores[i % 2], scores[(i + 1) % 2], top)


def gather_rows(ins, rows, part, target):
    for i, piece in enumerate(ins):
        target[i * rows : (i + 1) * rows] = piece[part]


def first_kernel(pieces, rows, *refs):
    ins, results = refs[:pieces], refs[pieces]
    queries, keys, values, one_scores, other_scores = refs[pieces + 1 :]
    for part, target in enumerate((queries, keys, values)):
        gather_rows(ins, rows, part, target)
    attend(queries, keys, values, results, (one_scores, other_scores), rows, True)


def second_kernel(pieces, rows, positions, *refs):
    count = len(positions)
    ins, earlier, outs = refs[:pieces], refs[pieces], refs[pieces + 1 : pieces + 1 + count]
    queries, keys, values, results, one_scores, other_scores = refs[pieces + 1 + count :]
    gather_rows(ins, rows, 1, keys)
    gather_rows(ins, rows, 2, values)
    gather_rows([ins[p] for p in positions], rows, 0, queries)
    attend(queries, keys, values, results, (one_scores, other_scores), rows, False)
    for i, position in enumerate(positions):
        outs[i][0] = earlier[position * rows : (position + 1) * rows]
        outs[i][1] = results[i * rows : (i + 1) * rows]


def join_kernel(*refs):
    for i, piece in enumerate(refs[:-1]):
        refs[-1][i] = piece[1]


def final_kernel(pieces, joins, flag, *refs):
    cached, back = refs[0], refs[1 : 1 + pieces]
    far, out, sems = refs[1 + pieces : 1 + pieces + len(joins)], refs[-2], refs[-1]
    me = lax.axis_index("seq")

    @pl.when(flag[0] > 0)
    def _():
        copies = []
        for join, offsets in enumerate(joins):
            for i, offset in enumerate(offsets):
                for group, piece in enumerate(
                    (back[offset].at[0], back[offset].at[1], far[join].at[i])
                ):
                    copies.append(
                        pltpu.make_async_copy(
                            piece,
                            out.at[0, :, head_columns(me, offset, group, pieces)],
                            sems.at[group, offset],
                        )
                    )
        run_copies(copies)

    @pl.when(flag[0] <= 0)
    def _():
        run_copies([pltpu.make_async_copy(cached, out, sems.at[0, 0])])


def body(query_rows, key_rows, value_rows, cached_rows, plan, timestep, assignment):
    pieces = lax.axis_size("seq")
    slots = lax.axis_size("batch")
    rows = query_rows.shape[1]
    group_width = pieces * HEAD_DIM
    order = ring(pieces)
    kind = query_rows.dtype
    dma = pltpu.SemaphoreType.DMA
    sources = (query_rows, key_rows, value_rows)

    def forward(value, offset):
        if offset == 0:
            return value
        return lax.ppermute(value, "seq", [(s, (s + offset) % pieces) for s in range(pieces)])

    def backward(value, offset):
        return forward(value, (pieces - offset) % pieces)

    def across(value):
        mask = slots // 2
        return lax.ppermute(value, "batch", [(s, s ^ mask) for s in range(slots)])

    def shape(*dims):
        return jax.ShapeDtypeStruct(dims, kind)

    def cost(blocks):
        pairs = blocks * rows * rows * pieces
        return pl.CostEstimate(
            flops=pairs * HEAD_DIM * 4,
            bytes_accessed=(2 * pieces + 2 * blocks) * rows * HEAD_DIM * 2,
            transcendentals=pairs,
        )

    far_out = pl.pallas_call(
        functools.partial(pack_far_kernel, group_width),
        out_shape=shape(3, rows, group_width),
        in_specs=[HBM] * 3,
        out_specs=VMEM,
        scratch_shapes=[dma((3,))],
        name="pack_far",
    )(*sources)
    far_in = across(far_out)

    def ordered(values, after):
        return lax.optimization_barrier((*values, after))[: len(values)]

    def pack_first(offsets, sources):
        return pl.pallas_call(
            functools.partial(pack_kernel, pieces, offsets),
            out_shape=[shape(3, rows, HEAD_DIM)] * len(offsets),
            in_specs=[HBM] * 3,
            out_specs=[VMEM] * len(offsets),
            scratch_shapes=[dma((len(offsets), 3))],
            name="pack_first",
        )(*sources)

    def pack_second(offsets, sources):
        return pl.pallas_call(
            functools.partial(pack_second_kernel, pieces, offsets),
            out_shape=[shape(3, rows, HEAD_DIM)] * len(offsets),
            in_specs=[SMEM] + [HBM] * 3 + [ANY],
            out_specs=[VMEM] * len(offsets),
            scratch_shapes=[dma((len(offsets), 3))],
            compiler_params=PACK,
            name="pack_second",
        )(flag, *sources, far_in)

    first_in = [None] * pieces
    for offsets, awaited in (([*order[:4], 0], None), ([order[4]], order[0]), ([order[5]], order[1]), ([order[6]], order[2])):
        values = sources if awaited is None else ordered(sources, first_in[awaited])
        for offset, value in zip(offsets, pack_first(offsets, values)):
            first_in[offset] = forward(value, offset)

    flag = pl.pallas_call(
        flag_kernel,
        out_shape=jax.ShapeDtypeStruct((1,), jnp.int32),
        in_specs=[SMEM] * 3,
        out_specs=SMEM,
        name="flag",
    )(*ordered((assignment, timestep, plan), first_in[order[2]]))

    second_in = [None] * pieces
    one, last, two, next_last, three, third_last, middle = order
    early, late = [last, two, next_last, three, third_last, middle, 0], [one]
    for offset, value in zip(early, pack_second(early, sources)):
        second_in[offset] = forward(value, offset)

    score_buffers = [pltpu.VMEM((rows, pieces * rows), jnp.float32)] * 2
    first_result = pl.pallas_call(
        functools.partial(first_kernel, pieces, rows),
        out_shape=shape(pieces * rows, HEAD_DIM),
        in_specs=[VMEM] * pieces,
        out_specs=VMEM,
        scratch_shapes=[pltpu.VMEM((pieces * rows, HEAD_DIM), kind)] * 3 + score_buffers,
        compiler_params=SHARED,
        cost_estimate=cost(pieces),
        name="attend_first",
    )(*ordered(first_in, second_in[last]))

    for offset, value in zip(late, pack_second(late, ordered(sources, first_result))):
        second_in[offset] = forward(value, offset)

    count = 2
    sends = [order[6], order[4], order[5], *order[2:4], *order[:2], 0]
    chunks = [sends[begin : begin + count] for begin in range(0, pieces, count)]
    back = [None] * pieces
    for offsets in chunks:
        results = pl.pallas_call(
            functools.partial(second_kernel, pieces, rows, offsets),
            out_shape=[shape(2, rows, HEAD_DIM)] * count,
            in_specs=[VMEM] * (pieces + 1),
            out_specs=[VMEM] * count,
            scratch_shapes=[
                pltpu.VMEM((count * rows, HEAD_DIM), kind),
                pltpu.VMEM((pieces * rows, HEAD_DIM), kind),
                pltpu.VMEM((pieces * rows, HEAD_DIM), kind),
                pltpu.VMEM((count * rows, HEAD_DIM), kind),
                *score_buffers,
            ],
            compiler_params=SHARED,
            cost_estimate=cost(count),
            name="attend_second",
        )(*second_in, first_result)
        for offset, value in zip(offsets, results):
            back[offset] = backward(value, offset)

    joins = [chunks[0] + chunks[1], *chunks[2:]]
    far_back = []
    for offsets in joins:
        joined = pl.pallas_call(
            join_kernel,
            out_shape=shape(len(offsets), rows, HEAD_DIM),
            in_specs=[VMEM] * len(offsets),
            out_specs=VMEM,
            compiler_params=SHARED,
            name="join",
        )(*[back[offset] for offset in offsets])
        far_back.append(across(joined))

    return pl.pallas_call(
        functools.partial(final_kernel, pieces, joins),
        out_shape=shape(*cached_rows.shape),
        in_specs=[SMEM, HBM] + [ANY] * (pieces + len(joins)),
        out_specs=ANY,
        scratch_shapes=[dma((GROUPS, pieces))],
        compiler_params=SHARED,
        name="final",
    )(flag, cached_rows, *back, *far_back)


def solution(mesh):
    rows = P("batch", "seq", None)
    return jax.shard_map(
        body,
        mesh=mesh,
        in_specs=(rows, rows, rows, rows, P(), P(), P()),
        out_specs=rows,
        check_vma=False,
    )
```

```python
import functools
import math

import jax
import jax.numpy as jnp
from jax import lax
from jax.experimental import pallas as pl
from jax.experimental.pallas import tpu as pltpu
from jax.sharding import PartitionSpec as P

HEAD_DIM = 128
GROUPS = 3
PACK = pltpu.CompilerParams(vmem_limit_bytes=58 << 20)
SHARED = pltpu.CompilerParams(vmem_limit_bytes=40 << 20)

ANY = pl.BlockSpec(memory_space=pl.ANY)
HBM = pl.BlockSpec(memory_space=pltpu.HBM)
VMEM = pl.BlockSpec(memory_space=pltpu.VMEM)
SMEM = pl.BlockSpec(memory_space=pltpu.SMEM)


def ring(pieces):
    half = pieces // 2
    return [step for near in range(1, half) for step in (near, pieces - near)] + [half]


def head_columns(me, offset, group, pieces):
    head = group * pieces + lax.rem(me + offset, pieces)
    return pl.ds(pl.multiple_of(head * HEAD_DIM, HEAD_DIM), HEAD_DIM)


def run_copies(copies):
    for copy in copies:
        copy.start()
    for copy in copies:
        copy.wait()


def pack_kernel(pieces, offsets, *refs):
    sources, outs, sems = refs[:3], refs[3:-1], refs[-1]
    me = lax.axis_index("seq")
    run_copies(
        [
            pltpu.make_async_copy(
                sources[part].at[0, :, head_columns(me, offset, 0, pieces)],
                outs[i].at[part],
                sems.at[i, part],
            )
            for i, offset in enumerate(offsets)
            for part in range(3)
        ]
    )


def pack_far_kernel(width, *refs):
    sources, out, sems = refs[:3], refs[3], refs[4]
    run_copies(
        [
            pltpu.make_async_copy(
                sources[part].at[0, :, pl.ds((GROUPS - 1) * width, width)], out.at[part], sems.at[part]
            )
            for part in range(3)
        ]
    )


def flag_kernel(assignment, timestep, plan, flag):
    request = assignment[lax.axis_index("batch")]
    flag[0] = plan[request, timestep[request]]


def pack_second_kernel(pieces, offsets, flag, *refs):
    sources, far = refs[:3], refs[3]
    outs, sems = refs[4:-1], refs[-1]
    me = lax.axis_index("seq")

    def move(own):
        run_copies(
            [
                pltpu.make_async_copy(
                    sources[part].at[0, :, head_columns(me, offset, 1, pieces)]
                    if own
                    else far.at[part, :, head_columns(me, offset, 0, pieces)],
                    outs[i].at[part],
                    sems.at[i, part],
                )
                for i, offset in enumerate(offsets)
                for part in range(3)
            ]
        )

    pl.when(flag[0] > 0)(lambda: move(True))
    pl.when(flag[0] <= 0)(lambda: move(False))


def attend(queries, keys, values, results, scores, block, looped):
    factor = math.log2(math.e) / math.sqrt(HEAD_DIM)
    total_keys = keys.shape[0]
    blocks = queries.shape[0] // block
    step = next(c for c in range(512, total_keys + 1, 128) if total_keys % c == 0)
    spans = [(begin, begin + step) for begin in range(0, total_keys, step)]

    def place(i):
        if isinstance(i, int):
            return pl.ds(i * block, block)
        return pl.ds(pl.multiple_of(i * block, block), block)

    def lanes(value):
        return [value[:, c : c + HEAD_DIM] for c in range(0, value.shape[1], HEAD_DIM)]

    def score(query, span, target, peak):
        part = lax.dot_general(
            query, keys[span[0] : span[1]], (((1,), (1,)), ((), ())), preferred_element_type=jnp.float32
        )
        target[:, span[0] : span[1]] = part
        return functools.reduce(jnp.maximum, lanes(part) + ([] if peak is None else [peak]))

    def weigh(source, span, top, total, mixed):
        shifted = jnp.exp2((source[:, span[0] : span[1]] - top) * factor)
        total = functools.reduce(jnp.add, lanes(shifted) + ([] if total is None else [total]))
        part = jnp.dot(
            shifted.astype(jnp.bfloat16), values[span[0] : span[1]], preferred_element_type=jnp.float32
        )
        return total, part if mixed is None else mixed + part

    def one(i, following, current, upcoming, top):
        peak = total = mixed = None
        if following is not None:
            query = queries[place(following)]
        for span in spans:
            if following is not None:
                peak = score(query, span, upcoming, peak)
            total, mixed = weigh(current, span, top, total, mixed)
        results[place(i)] = (mixed / jnp.sum(total, axis=1, keepdims=True)).astype(jnp.bfloat16)
        return None if following is None else jnp.max(peak, axis=1, keepdims=True)

    peak = None
    query = queries[place(0)]
    for span in spans:
        peak = score(query, span, scores[0], peak)
    top = jnp.max(peak, axis=1, keepdims=True)
    if looped:

        def pair(i, top):
            top = one(2 * i, 2 * i + 1, scores[0], scores[1], top)
            return one(2 * i + 1, jnp.minimum(2 * i + 2, blocks - 1), scores[1], scores[0], top)

        lax.fori_loop(0, blocks // 2, pair, top)
    else:
        for i in range(blocks):
            following = i + 1 if i + 1 < blocks else None
            top = one(i, following, scores[i % 2], scores[(i + 1) % 2], top)


def gather_rows(ins, rows, part, target):
    for i, piece in enumerate(ins):
        target[i * rows : (i + 1) * rows] = piece[part]


def first_kernel(pieces, rows, *refs):
    ins, results = refs[:pieces], refs[pieces]
    queries, keys, values, one_scores, other_scores = refs[pieces + 1 :]
    for part, target in enumerate((queries, keys, values)):
        gather_rows(ins, rows, part, target)
    attend(queries, keys, values, results, (one_scores, other_scores), rows, True)


def second_kernel(pieces, rows, positions, *refs):
    count = len(positions)
    ins, earlier, outs = refs[:pieces], refs[pieces], refs[pieces + 1 : pieces + 1 + count]
    queries, keys, values, results, one_scores, other_scores = refs[pieces + 1 + count :]
    gather_rows(ins, rows, 1, keys)
    gather_rows(ins, rows, 2, values)
    gather_rows([ins[p] for p in positions], rows, 0, queries)
    attend(queries, keys, values, results, (one_scores, other_scores), rows, False)
    for i, position in enumerate(positions):
        outs[i][0] = earlier[position * rows : (position + 1) * rows]
        outs[i][1] = results[i * rows : (i + 1) * rows]


def join_kernel(*refs):
    for i, piece in enumerate(refs[:-1]):
        refs[-1][i] = piece[1]


def final_kernel(pieces, joins, flag, *refs):
    cached, back = refs[0], refs[1 : 1 + pieces]
    far, out, sems = refs[1 + pieces : 1 + pieces + len(joins)], refs[-2], refs[-1]
    me = lax.axis_index("seq")

    @pl.when(flag[0] > 0)
    def _():
        copies = []
        for join, offsets in enumerate(joins):
            for i, offset in enumerate(offsets):
                for group, piece in enumerate(
                    (back[offset].at[0], back[offset].at[1], far[join].at[i])
                ):
                    copies.append(
                        pltpu.make_async_copy(
                            piece,
                            out.at[0, :, head_columns(me, offset, group, pieces)],
                            sems.at[group, offset],
                        )
                    )
        run_copies(copies)

    @pl.when(flag[0] <= 0)
    def _():
        run_copies([pltpu.make_async_copy(cached, out, sems.at[0, 0])])


def body(query_rows, key_rows, value_rows, cached_rows, plan, timestep, assignment):
    pieces = lax.axis_size("seq")
    slots = lax.axis_size("batch")
    rows = query_rows.shape[1]
    group_width = pieces * HEAD_DIM
    order = ring(pieces)
    kind = query_rows.dtype
    dma = pltpu.SemaphoreType.DMA
    sources = (query_rows, key_rows, value_rows)

    def forward(value, offset):
        if offset == 0:
            return value
        return lax.ppermute(value, "seq", [(s, (s + offset) % pieces) for s in range(pieces)])

    def backward(value, offset):
        return forward(value, (pieces - offset) % pieces)

    def across(value):
        mask = slots // 2
        return lax.ppermute(value, "batch", [(s, s ^ mask) for s in range(slots)])

    def shape(*dims):
        return jax.ShapeDtypeStruct(dims, kind)

    def cost(blocks):
        pairs = blocks * rows * rows * pieces
        return pl.CostEstimate(
            flops=pairs * HEAD_DIM * 4,
            bytes_accessed=(2 * pieces + 2 * blocks) * rows * HEAD_DIM * 2,
            transcendentals=pairs,
        )

    far_out = pl.pallas_call(
        functools.partial(pack_far_kernel, group_width),
        out_shape=shape(3, rows, group_width),
        in_specs=[HBM] * 3,
        out_specs=VMEM,
        scratch_shapes=[dma((3,))],
        name="pack_far",
    )(*sources)
    far_in = across(far_out)

    def ordered(values, after):
        return lax.optimization_barrier((*values, after))[: len(values)]

    def pack_first(offsets, sources):
        return pl.pallas_call(
            functools.partial(pack_kernel, pieces, offsets),
            out_shape=[shape(3, rows, HEAD_DIM)] * len(offsets),
            in_specs=[HBM] * 3,
            out_specs=[VMEM] * len(offsets),
            scratch_shapes=[dma((len(offsets), 3))],
            name="pack_first",
        )(*sources)

    def pack_second(offsets, sources):
        return pl.pallas_call(
            functools.partial(pack_second_kernel, pieces, offsets),
            out_shape=[shape(3, rows, HEAD_DIM)] * len(offsets),
            in_specs=[SMEM] + [HBM] * 3 + [ANY],
            out_specs=[VMEM] * len(offsets),
            scratch_shapes=[dma((len(offsets), 3))],
            compiler_params=PACK,
            name="pack_second",
        )(flag, *sources, far_in)

    first_in = [None] * pieces
    for offsets, awaited in (([*order[:4], 0], None), ([order[4]], order[0]), ([order[5]], order[1]), ([order[6]], order[2])):
        values = sources if awaited is None else ordered(sources, first_in[awaited])
        for offset, value in zip(offsets, pack_first(offsets, values)):
            first_in[offset] = forward(value, offset)

    flag = pl.pallas_call(
        flag_kernel,
        out_shape=jax.ShapeDtypeStruct((1,), jnp.int32),
        in_specs=[SMEM] * 3,
        out_specs=SMEM,
        name="flag",
    )(*ordered((assignment, timestep, plan), first_in[order[2]]))

    second_in = [None] * pieces
    one, last, two, next_last, three, third_last, middle = order
    early, late = [last, two, next_last, three, third_last, middle, 0], [one]
    for offsets in (early[:2], early[2:]):
        for offset, value in zip(offsets, pack_second(offsets, sources)):
            second_in[offset] = forward(value, offset)

    score_buffers = [pltpu.VMEM((rows, pieces * rows), jnp.float32)] * 2
    first_result = pl.pallas_call(
        functools.partial(first_kernel, pieces, rows),
        out_shape=shape(pieces * rows, HEAD_DIM),
        in_specs=[VMEM] * pieces,
        out_specs=VMEM,
        scratch_shapes=[pltpu.VMEM((pieces * rows, HEAD_DIM), kind)] * 3 + score_buffers,
        compiler_params=SHARED,
        cost_estimate=cost(pieces),
        name="attend_first",
    )(*ordered(first_in, second_in[last]))

    for offset, value in zip(late, pack_second(late, ordered(sources, first_result))):
        second_in[offset] = forward(value, offset)

    count = 2
    sends = [order[6], order[4], order[5], *order[2:4], *order[:2], 0]
    chunks = [sends[begin : begin + count] for begin in range(0, pieces, count)]
    back = [None] * pieces
    for offsets in chunks:
        results = pl.pallas_call(
            functools.partial(second_kernel, pieces, rows, offsets),
            out_shape=[shape(2, rows, HEAD_DIM)] * count,
            in_specs=[VMEM] * (pieces + 1),
            out_specs=[VMEM] * count,
            scratch_shapes=[
                pltpu.VMEM((count * rows, HEAD_DIM), kind),
                pltpu.VMEM((pieces * rows, HEAD_DIM), kind),
                pltpu.VMEM((pieces * rows, HEAD_DIM), kind),
                pltpu.VMEM((count * rows, HEAD_DIM), kind),
                *score_buffers,
            ],
            compiler_params=SHARED,
            cost_estimate=cost(count),
            name="attend_second",
        )(*second_in, first_result)
        for offset, value in zip(offsets, results):
            back[offset] = backward(value, offset)

    joins = [chunks[0] + chunks[1], *chunks[2:]]
    far_back = []
    for offsets in joins:
        joined = pl.pallas_call(
            join_kernel,
            out_shape=shape(len(offsets), rows, HEAD_DIM),
            in_specs=[VMEM] * len(offsets),
            out_specs=VMEM,
            compiler_params=SHARED,
            name="join",
        )(*[back[offset] for offset in offsets])
        far_back.append(across(joined))

    return pl.pallas_call(
        functools.partial(final_kernel, pieces, joins),
        out_shape=shape(*cached_rows.shape),
        in_specs=[SMEM, HBM] + [ANY] * (pieces + len(joins)),
        out_specs=ANY,
        scratch_shapes=[dma((GROUPS, pieces))],
        compiler_params=SHARED,
        name="final",
    )(flag, cached_rows, *back, *far_back)


def solution(mesh):
    rows = P("batch", "seq", None)
    return jax.shard_map(
        body,
        mesh=mesh,
        in_specs=(rows, rows, rows, rows, P(), P(), P()),
        out_specs=rows,
        check_vma=False,
    )
```
